512 devices in a mesh: img: 8 (over x, core), atom: 64 (over z, y).
Axes of the slice: x: 4, y: 8, z: 8, core: 2. Of those that a mesh axis runs over, the one named last changes fastest.
Arguments:
- density: bfloat16 [8, 9, 9, 196608], P('img', None, None, 'atom'), may hold values from -1.5 to 1.5
- energy_density: bfloat16 [8, 9, 9, 196608], P('img', None, None, 'atom'), may hold values from -1.5 to 1.5
- dham: bfloat16 [8, 3, 9, 9, 196608], P('img', None, None, None, 'atom'), may hold values from -1.5 to 1.5
- dovl: bfloat16 [8, 3, 9, 9, 196608], P('img', None, None, None, 'atom'), may hold values from -1.5 to 1.5
- pair_owner: int32 [8, 196608], P('img', 'atom'), may hold values from 0 to 511
- pair_partner: int32 [8, 196608], P('img', 'atom'), may hold values from 0 to 32767, as said below
- partner_species: int32 [8, 196608], P('img', 'atom'), may hold values from 0 to 3, as said below
- pair_count: int32 [8, 64], P('img', 'atom'), may hold values from 768 to 3072, as said below
- species: int32 [32768], P('atom'), may hold values from 0 to 3
- orbitals: int32 [4], replicated, may hold values from 1 to 9, as said below
- coords: float32 [8, 3, 32768], P('img', None, 'atom')
- reactant: float32 [3, 32768], P(None, 'atom')
- product: float32 [3, 32768], P(None, 'atom')
Outputs:
- band_force: float32 [8, 3, 32768], P('img', None, 'atom')
- tangent_force: float32 [8], P('img')
The draws below stay inside these ranges and needn't reach their ends.
Inputs may be any that keep to these rules, and one draw needn't show every extreme that they name: `pair_count`: each owner's live slots are its first ones; in every image some owner has all 3072 slots live, and every owner at least a quarter of them. partner_species[i, p] equals species[pair_partner[i, p]]. `pair_partner`: partners may be any atoms of the image; the first slot of owner o has its partner among the atoms of owner (o + 32) modulo 64 (owner o holds atoms o * 512 to o * 512 + 511). Species 0 has all 9 orbitals and the last species one.
All inputs are finite; a program needn't handle non-finite values.
Results may differ from the reference program's by a relative error of at most 0.0003.
Values sent between devices are 32-bit elements; how exact they have to be, the bound alone decides.
No kernel may reach another device: no remote copies, remote signals or barrier semaphores. Data moves between devices by JAX's collectives and lax.ppermute only.
A program may use at most 64 MiB of HBM per device.

```python
import jax
import jax.numpy as jnp
from jax import lax

ORB = 9
SPECIES = 4
A_DEV = 512
P_DEV = 3072
IMAGES = 8
OWNERS = 64
ATOMS = 32768
PAIRS = 196608


def pair_lists(key):
    kinds = jax.random.randint(jax.random.fold_in(key, 101), (ATOMS,), 0, SPECIES).astype(jnp.int32)
    slots = jnp.arange(PAIRS, dtype=jnp.int32)
    owner_index = (slots // P_DEV).astype(jnp.int32)
    first_slot = slots % P_DEV == 0
    drawn_owner = jax.random.randint(jax.random.fold_in(key, 103), (IMAGES, PAIRS), 0, OWNERS).astype(jnp.int32)
    far_owner = jnp.mod(owner_index + OWNERS // 2, OWNERS).astype(jnp.int32)
    target = jnp.where(first_slot[None, :], far_owner[None, :], drawn_owner).astype(jnp.int32)
    within = jax.random.randint(jax.random.fold_in(key, 102), (IMAGES, PAIRS), 0, A_DEV).astype(jnp.int32)
    partners = (target * A_DEV + within).astype(jnp.int32)
    return (kinds, partners, kinds[partners])


def draw_species(key, part):
    return pair_lists(key)[0]


def draw_pair_partner(key, part):
    return pair_lists(key)[1]


def draw_partner_species(key, part):
    return pair_lists(key)[2]


def draw_pair_count(key, part):
    counts = jax.random.randint(jax.random.fold_in(key, 51), (IMAGES, OWNERS), P_DEV // 4, P_DEV + 1)
    chosen = jax.random.randint(jax.random.fold_in(key, 52), (IMAGES, 1), 0, OWNERS)
    owners_index = jnp.arange(OWNERS, dtype=jnp.int32)[None, :]
    return jnp.where(owners_index == chosen, P_DEV, counts).astype(jnp.int32)


def draw_orbitals(key, part):
    middle = jax.random.randint(jax.random.fold_in(key, 61), (SPECIES - 2,), 1, ORB + 1)
    return jnp.concatenate([jnp.full((1,), ORB), middle, jnp.ones((1,))]).astype(jnp.int32)


def band_point(key, index):
    base = 4.0 * jax.random.normal(jax.random.fold_in(key, 31), (3, ATOMS), jnp.float32)
    place = jnp.arange(ATOMS, dtype=jnp.float32) / max(ATOMS - 1, 1)
    image_key = jax.random.fold_in(jax.random.fold_in(key, 37), index)
    image_scale = jnp.exp(jax.random.uniform(image_key, (), jnp.float32, -0.7, 0.7))
    noise_key = jax.random.fold_in(jax.random.fold_in(key, 41), index)
    rise = 3.0 ** (0.5 * place)
    noise = jax.random.normal(noise_key, (3, ATOMS), jnp.float32)
    return base + 0.3 * image_scale * rise[None, :] * noise


def draw_coords(key, part):
    return jnp.stack([band_point(key, index) for index in range(IMAGES)], axis=0)


def draw_reactant(key, part):
    return band_point(key, 1000)


def draw_product(key, part):
    return band_point(key, 1001)


def touch_ends(values, stream_key, low, high):
    spot = [jax.random.randint(jax.random.fold_in(stream_key, axis), (), 0, length) for axis, length in enumerate(values.shape)]
    main_axis = values.shape.index(max(values.shape))
    beside = spot[:main_axis] + [(spot[main_axis] + 1) % values.shape[main_axis]] + spot[main_axis + 1:]
    return values.at[tuple(spot)].set(low).at[tuple(beside)].set(high)


def block_scale(own_key, extent, split, least, top_value):
    def one(axis_at, blocks):
        draws = jax.random.uniform(jax.random.fold_in(jax.random.fold_in(own_key, 6), axis_at), (blocks,), jnp.float32, least / len(split), top_value / len(split))
        return jnp.repeat(jnp.exp(draws), extent[axis_at] // blocks).reshape((-1,) + (1,) * (len(extent) - axis_at - 1))

    loudness = one(*split[0])
    for cut in split[1:]:
        loudness = loudness * one(*cut)
    return loudness


def normal_values(rng, extent, width, reach, pieces=(), kind=jnp.bfloat16):
    gain = block_scale(rng, extent, pieces, -0.22, 0.18) if pieces else 1.0
    drawn = jax.random.normal(rng, extent, jnp.float32) * width * gain
    return jnp.minimum(jnp.maximum(drawn, -reach), reach).astype(kind)


def setup_inputs(seed: int = 0) -> dict:
    keys = jax.random.split(jax.random.key(seed), 14)
    return {
        "density": normal_values(keys[0], (IMAGES, ORB, ORB, PAIRS), 0.25, 1.5, ((0, 8), (3, 64))),
        "energy_density": normal_values(keys[1], (IMAGES, ORB, ORB, PAIRS), 0.25, 1.5, ((0, 8), (3, 64))),
        "dham": normal_values(keys[2], (IMAGES, 3, ORB, ORB, PAIRS), 0.25, 1.5, ((0, 8), (4, 64))),
        "dovl": normal_values(keys[3], (IMAGES, 3, ORB, ORB, PAIRS), 0.25, 1.5, ((0, 8), (4, 64))),
        "pair_owner": touch_ends(jax.random.randint(keys[4], (IMAGES, PAIRS), 0, A_DEV), jax.random.fold_in(keys[4], 1), 0, A_DEV - 1).astype(jnp.int32),
        "pair_partner": draw_pair_partner(jax.random.fold_in(keys[13], 71), 0),
        "partner_species": draw_partner_species(jax.random.fold_in(keys[13], 71), 0),
        "pair_count": draw_pair_count(jax.random.fold_in(keys[13], 71), 0),
        "species": draw_species(jax.random.fold_in(keys[13], 71), 0),
        "orbitals": draw_orbitals(jax.random.fold_in(keys[13], 71), 0),
        "coords": draw_coords(jax.random.fold_in(keys[13], 71), 0),
        "reactant": draw_reactant(jax.random.fold_in(keys[13], 71), 0),
        "product": draw_product(jax.random.fold_in(keys[13], 71), 0),
    }


spring_const = 1.0
tangent_eps = 1e-06

def image_forces(items, species, orbitals):
    dens, energy, dham_img, dovl_img, owner, partner, partner_kind, count = items
    slots = jnp.arange(PAIRS, dtype=jnp.int32)
    device = (slots // P_DEV).astype(jnp.int32)
    live = slots % P_DEV < count[device]
    owner_atom = (device * A_DEV + owner).astype(jnp.int32)
    own_orbitals = orbitals[species[owner_atom]]
    partner_orbitals = orbitals[partner_kind]
    levels = jnp.arange(ORB, dtype=jnp.int32)
    row_ok = (levels[:, None] < own_orbitals[None, :]) & live[None, :]
    col_ok = levels[:, None] < partner_orbitals[None, :]
    mask = (row_ok[:, None, :] & col_ok[None, :, :]).astype(jnp.bfloat16)
    masked_density = dens * mask
    masked_energy = energy * mask
    term_ham = jnp.einsum('abp,cabp->cp', masked_density.astype(jnp.float32), dham_img.astype(jnp.float32))
    term_ovl = jnp.einsum('abp,cabp->cp', masked_energy.astype(jnp.float32), dovl_img.astype(jnp.float32))
    pair_force = -2.0 * (term_ham - term_ovl)
    total = jnp.zeros((3, ATOMS), jnp.float32)
    total = total.at[:, owner_atom].add(pair_force)
    total = total.at[:, partner].add(-pair_force)
    return total

def reference(density, energy_density, dham, dovl, pair_owner, pair_partner, partner_species, pair_count, species, orbitals, coords, reactant, product):
    items = (density, energy_density, dham, dovl, pair_owner, pair_partner, partner_species, pair_count)
    force = lax.map(lambda entry: image_forces(entry, species, orbitals), items)
    prior = jnp.concatenate([reactant[None], coords[:-1]], axis=0)
    later = jnp.concatenate([coords[1:], product[None]], axis=0)
    tangent = later - prior
    ahead = lax.optimization_barrier(jnp.sum((later - coords) ** 2, axis=(1, 2)))
    behind = lax.optimization_barrier(jnp.sum((coords - prior) ** 2, axis=(1, 2)))
    length = lax.optimization_barrier(jnp.sum(tangent * tangent, axis=(1, 2)))
    unit = tangent / jnp.sqrt(length + tangent_eps)[:, None, None]
    tangent_force = lax.optimization_barrier(jnp.sum(force * unit, axis=(1, 2)))
    spring = spring_const * (jnp.sqrt(ahead) - jnp.sqrt(behind))
    band_force = force - tangent_force[:, None, None] * unit + spring[:, None, None] * unit
    return (band_force, tangent_force)
```

```python
import jax
import jax.numpy as jnp
from jax import lax
from jax.experimental import pallas as pl
from jax.experimental.pallas import tpu as pltpu
from jax.sharding import PartitionSpec as P

spring_const = 1.0
tangent_eps = 1e-06
LANES = 128
CHUNK = 512

VMEM = pl.BlockSpec(memory_space=pltpu.VMEM)
SMEM = pl.BlockSpec(memory_space=pltpu.SMEM)


def cost(flops, moved):
    return pl.CostEstimate(flops=flops, bytes_accessed=moved, transcendentals=0)


def passed_along(block, axis, distance):
    devices = range(lax.axis_size(axis))
    route = [(i - distance, i) for i in devices if i - distance in devices]
    return lax.ppermute(block, axis, route)


def limits_kernel(
    orbitals_ref, count_ref, species_ref, owner_ref, partner_kind_ref, own_ref, other_ref
):
    def orbitals_of(kind):
        found = jnp.zeros_like(kind)
        for k in range(orbitals_ref.shape[0]):
            found = jnp.where(kind == k, orbitals_ref[k], found)
        return found

    rows = owner_ref.shape[0]
    table = orbitals_of(species_ref[...])
    owner = owner_ref[...]
    block, lane = owner // LANES, owner % LANES
    own = jnp.zeros_like(owner)
    for q in range(table.shape[0]):
        row = jnp.broadcast_to(table[q : q + 1, :], (rows, LANES))
        own = jnp.where(block == q, jnp.take_along_axis(row, lane, axis=1), own)
    slot = lax.broadcasted_iota(jnp.int32, (rows, LANES), 0) * LANES
    slot = slot + lax.broadcasted_iota(jnp.int32, (rows, LANES), 1)
    own_ref[...] = jnp.where(slot < count_ref[0, 0], own, 0)
    other_ref[...] = orbitals_of(partner_kind_ref[...])


def two_pieces(value):
    high = value.astype(jnp.bfloat16)
    low = (value - high.astype(jnp.float32)).astype(jnp.bfloat16)
    return high, low


def product_nt(a, b):
    return lax.dot_general(
        a, b, (((1,), (1,)), ((), ())), preferred_element_type=jnp.float32
    )


def scatter_kernel(blocks, owners, force_ref, owner_ref, partner_ref, sent_ref, own_ref):
    n_slots = force_ref.shape[1]
    local = blocks * LANES
    total = jnp.zeros((blocks * owners, 3 * LANES), jnp.float32)
    own_total = jnp.zeros((2 * 3 * blocks, LANES), jnp.float32)
    for start in range(0, n_slots, CHUNK):
        span = pl.ds(start, CHUNK)
        partner = partner_ref[:, span]
        row = (partner % local) // LANES * owners + partner // local
        rows = lax.broadcasted_iota(jnp.int32, (blocks * owners, CHUNK), 0)
        choose_row = jnp.where(rows == row, 1.0, 0.0).astype(jnp.bfloat16)
        lanes = lax.broadcasted_iota(jnp.int32, (LANES, CHUNK), 0)
        at_lane = lanes == partner % LANES
        force = force_ref[:, span]
        high, low = two_pieces(force)
        high32, low32 = high.astype(jnp.float32), low.astype(jnp.float32)
        for piece in (high32, low32):
            spread = jnp.concatenate(
                [jnp.where(at_lane, piece[c : c + 1, :], 0.0) for c in range(3)], axis=0
            ).astype(jnp.bfloat16)
            total = total + product_nt(choose_row, spread)
        owner = owner_ref[:, span]
        own_lane = jnp.where(lanes == owner % LANES, 1.0, 0.0).astype(jnp.bfloat16)
        blocks_at = lax.broadcasted_iota(jnp.int32, (blocks, CHUNK), 0) == owner // LANES
        own_rows = jnp.concatenate(
            [
                jnp.where(blocks_at, piece[c : c + 1, :], 0.0)
                for piece in (high32, low32)
                for c in range(3)
            ],
            axis=0,
        ).astype(jnp.bfloat16)
        own_total = own_total + product_nt(own_rows, own_lane)
    for c in range(3):
        for q in range(blocks):
            sent_ref[pl.ds(c * blocks + q, owners, stride=3 * blocks), :] = -total[
                q * owners : (q + 1) * owners, c * LANES : (c + 1) * LANES
            ]
    own_ref[...] = own_total[: 3 * blocks, :] + own_total[3 * blocks :, :]


def force_kernel(
    blocks, owners, images,
    image_ref, got_ref, own_ref, now_ref, prior_ref, later_ref, first_ref, last_ref,
    force_ref, tangent_ref, parts_ref,
):
    is_first = image_ref[0] == 0
    is_last = image_ref[0] == images - 1
    zero = jnp.zeros((1, LANES), jnp.float32)
    ahead, behind, length, along = zero, zero, zero, zero
    for c in range(3):
        for q in range(blocks):
            k = c * blocks + q
            at = pl.ds(q * LANES, LANES)
            now = now_ref[c, :, at]
            prior = jnp.where(is_first, first_ref[c : c + 1, at], prior_ref[c, :, at])
            later = jnp.where(is_last, last_ref[c : c + 1, at], later_ref[c, :, at])
            tangent = later - prior
            got = got_ref[pl.ds(k, owners, stride=3 * blocks), :]
            force = own_ref[k : k + 1, :] + jnp.sum(got, axis=0, keepdims=True)
            ahead = ahead + (later - now) ** 2
            behind = behind + (now - prior) ** 2
            length = length + tangent * tangent
            along = along + force * tangent
            force_ref[k : k + 1, :] = force
            tangent_ref[k : k + 1, :] = tangent
    place = lax.broadcasted_iota(jnp.int32, (1, LANES), 1)
    parts = zero
    for at, part in enumerate((ahead, behind, length, along)):
        parts = jnp.where(place == at, jnp.sum(part, axis=1, keepdims=True), parts)
    parts_ref[...] = jnp.broadcast_to(parts, parts_ref.shape)


def band_kernel(blocks, parts_ref, force_ref, tangent_ref, band_ref, along_ref):
    parts = jnp.sum(parts_ref[...], axis=0, keepdims=True)
    ahead, behind, length, along = (parts[:, at : at + 1] for at in range(4))
    root = jnp.sqrt(length + tangent_eps)
    along = along / root
    spring = spring_const * (jnp.sqrt(ahead) - jnp.sqrt(behind))
    push = spring - along
    for c in range(3):
        for q in range(blocks):
            k = c * blocks + q
            unit = tangent_ref[k : k + 1, :] / root
            band_ref[c, :, pl.ds(q * LANES, LANES)] = force_ref[k : k + 1, :] + push * unit
    along_ref[...] = jnp.broadcast_to(along, along_ref.shape)


def local(
    density,
    energy_density,
    dham,
    dovl,
    pair_owner,
    pair_partner,
    partner_species,
    pair_count,
    species,
    orbitals,
    coords,
    reactant,
    product,
):
    n_slots = density.shape[-1]
    n_orbit = density.shape[1]
    atoms_local = species.shape[0]
    blocks = atoms_local // LANES
    owners = lax.axis_size("atom")
    images = lax.axis_size("img")
    rows = 3 * blocks
    f32, i32 = jnp.float32, jnp.int32

    current = jnp.transpose(coords, (1, 0, 2))
    before = passed_along(current, "img", 1)
    after = passed_along(current, "img", -1)

    own_orbitals, partner_orbitals = pl.pallas_call(
        limits_kernel,
        out_shape=[jax.ShapeDtypeStruct((n_slots // LANES, LANES), i32)] * 2,
        in_specs=[SMEM, SMEM, VMEM, VMEM, VMEM],
        out_specs=[VMEM, VMEM],
        compiler_params=pltpu.CompilerParams(vmem_limit_bytes=16 << 20),
        cost_estimate=cost(10 * n_slots, 16 * n_slots),
        name="limits",
    )(
        orbitals,
        pair_count,
        species.reshape(blocks, LANES),
        pair_owner.reshape(-1, LANES),
        partner_species.reshape(-1, LANES),
    )
    own_orbitals = own_orbitals.reshape(n_slots)
    partner_orbitals = partner_orbitals.reshape(n_slots)
    levels = jnp.arange(n_orbit, dtype=jnp.int32)
    row_ok = levels[:, None] < own_orbitals[None, :]
    col_ok = levels[:, None] < partner_orbitals[None, :]
    mask = (row_ok[:, None, :] & col_ok[None, :, :]).astype(jnp.bfloat16)
    masked_density = density[0] * mask
    masked_energy = energy_density[0] * mask
    term_ham = jnp.einsum(
        "abp,cabp->cp", masked_density, dham[0], preferred_element_type=jnp.float32
    )
    term_ovl = jnp.einsum(
        "abp,cabp->cp", masked_energy, dovl[0], preferred_element_type=jnp.float32
    )
    pair_force = -2.0 * (term_ham - term_ovl)

    sent, own = pl.pallas_call(
        lambda *refs: scatter_kernel(blocks, owners, *refs),
        out_shape=[
            jax.ShapeDtypeStruct((owners * rows, LANES), f32),
            jax.ShapeDtypeStruct((rows, LANES), f32),
        ],
        in_specs=[VMEM] * 3,
        out_specs=[VMEM] * 2,
        compiler_params=pltpu.CompilerParams(vmem_limit_bytes=16 << 20),
        cost_estimate=cost(4 * n_slots * owners * rows * LANES, 4 * owners * rows * LANES),
        name="scatter",
    )(pair_force, pair_owner, pair_partner)
    got = lax.all_to_all(sent.reshape(owners, rows * LANES), "atom", 0, 0, tiled=True)

    force, tangent, parts = pl.pallas_call(
        lambda *refs: force_kernel(blocks, owners, images, *refs),
        out_shape=[
            jax.ShapeDtypeStruct((rows, LANES), f32),
            jax.ShapeDtypeStruct((rows, LANES), f32),
            jax.ShapeDtypeStruct((owners, LANES), f32),
        ],
        in_specs=[SMEM] + [VMEM] * 7,
        out_specs=[VMEM] * 3,
        compiler_params=pltpu.CompilerParams(vmem_limit_bytes=16 << 20),
        cost_estimate=cost(owners * rows * LANES, 4 * owners * rows * LANES),
        name="force",
    )(
        lax.axis_index("img").astype(i32).reshape(1),
        got.reshape(owners * rows, LANES),
        own,
        current,
        before,
        after,
        reactant,
        product,
    )
    parts = lax.all_to_all(parts, "atom", 0, 0, tiled=True)
    band, along = pl.pallas_call(
        lambda *refs: band_kernel(blocks, *refs),
        out_shape=[
            jax.ShapeDtypeStruct((3, 1, atoms_local), f32),
            jax.ShapeDtypeStruct((1, LANES), f32),
        ],
        in_specs=[VMEM] * 3,
        out_specs=[VMEM] * 2,
        compiler_params=pltpu.CompilerParams(vmem_limit_bytes=16 << 20),
        cost_estimate=cost(owners * LANES, 4 * owners * LANES),
        name="band",
    )(parts, force, tangent)
    return (jnp.transpose(band, (1, 0, 2)), along[0, :1])


def solution(mesh):
    return jax.shard_map(
        local,
        mesh=mesh,
        in_specs=(
            P("img", None, None, "atom"),
            P("img", None, None, "atom"),
            P("img", None, None, None, "atom"),
            P("img", None, None, None, "atom"),
            P("img", "atom"),
            P("img", "atom"),
            P("img", "atom"),
            P("img", "atom"),
            P("atom"),
            P(),
            P("img", None, "atom"),
            P(None, "atom"),
            P(None, "atom"),
        ),
        out_specs=(P("img", None, "atom"), P("img")),
        check_vma=False,
    )
```

```python
import jax
import jax.numpy as jnp
from jax import lax
from jax.experimental import pallas as pl
from jax.experimental.pallas import tpu as pltpu
from jax.sharding import PartitionSpec as P

spring_const = 1.0
tangent_eps = 1e-06
LANES = 128
CHUNK = 512
DEPTH = 2

VMEM = pl.BlockSpec(memory_space=pltpu.VMEM)
SMEM = pl.BlockSpec(memory_space=pltpu.SMEM)
HBM = pl.BlockSpec(memory_space=pltpu.HBM)


def cost(flops, moved):
    return pl.CostEstimate(flops=flops, bytes_accessed=moved, transcendentals=0)


def passed_along(block, axis, distance):
    devices = range(lax.axis_size(axis))
    route = [(i - distance, i) for i in devices if i - distance in devices]
    return lax.ppermute(block, axis, route)


def product_nt(a, b):
    return lax.dot_general(
        a, b, (((1,), (1,)), ((), ())), preferred_element_type=jnp.float32
    )


def pairs_kernel(
    blocks, owners,
    count_ref, orbitals_hbm, species_hbm, owner_hbm, partner_hbm, kind_hbm,
    density_hbm, energy_hbm, dham_hbm, dovl_hbm,
    sent_ref,
    orbitals_ref, species_ref, owner_ref, partner_ref, kind_ref,
    density_ref, energy_ref, dham_ref, dovl_ref,
    force_ref, weight_ref, energy_weight_ref, row_ref, lane_ref, own_lane_ref,
    total_ref, own_total_ref, small_sem, block_sem,
):
    f32, bf16, i32 = jnp.float32, jnp.bfloat16, jnp.int32
    n_orbit, _, n_slots = density_ref.shape
    steps = n_slots // CHUNK
    small = [
        pltpu.make_async_copy(source, target, small_sem.at[i])
        for i, (source, target) in enumerate(
            (
                (orbitals_hbm, orbitals_ref),
                (species_hbm, species_ref),
                (owner_hbm, owner_ref),
                (partner_hbm, partner_ref),
                (kind_hbm, kind_ref),
            )
        )
    ]
    for copy in small:
        copy.start()
    spans = [pl.ds(step * CHUNK, CHUNK) for step in range(steps)]
    streams = []
    for step, at in enumerate(spans):
        pieces = (
            (density_hbm.at[0, :, :, at], density_ref.at[:, :, at]),
            (energy_hbm.at[0, :, :, at], energy_ref.at[:, :, at]),
            (dham_hbm.at[0, :, :, :, at], dham_ref.at[:, :, :, at]),
            (dovl_hbm.at[0, :, :, :, at], dovl_ref.at[:, :, :, at]),
        )
        streams.append(
            [
                pltpu.make_async_copy(source, target, block_sem.at[i, step])
                for i, (source, target) in enumerate(pieces)
            ]
        )
    for step in range(DEPTH):
        for copy in streams[step]:
            copy.start()
    for copy in small:
        copy.wait()

    def orbitals_of(kind):
        found = jnp.zeros_like(kind)
        for k in range(orbitals_ref.shape[0]):
            found = jnp.where(kind == k, orbitals_ref[k], found)
        return found

    table = orbitals_of(species_ref[...]).astype(f32)
    table = jnp.concatenate([table, jnp.zeros((8 - blocks, LANES), f32)], axis=0).astype(bf16)
    local = blocks * LANES
    limits = []
    for step, at in enumerate(spans):
        owner, partner = owner_ref[:, at], partner_ref[:, at]
        lanes = lax.broadcasted_iota(i32, (LANES, CHUNK), 0)
        own_lane = jnp.where(lanes == owner % LANES, 1.0, 0.0).astype(bf16)
        own_lane_ref[:, at] = own_lane
        lane_ref[:, at] = jnp.where(lanes == partner % LANES, 1.0, 0.0).astype(bf16)
        row = (partner % local) // LANES * owners + partner // local
        rows = lax.broadcasted_iota(i32, (blocks * owners, CHUNK), 0)
        row_ref[:, at] = jnp.where(rows == row, 1.0, 0.0).astype(bf16)
        look = lax.dot_general(
            table, own_lane, (((1,), (0,)), ((), ())), preferred_element_type=f32
        )
        at_block = lax.broadcasted_iota(i32, (8, CHUNK), 0) == owner // LANES
        own = jnp.sum(jnp.where(at_block, look, 0.0), axis=0, keepdims=True).astype(i32)
        slot = step * CHUNK + lax.broadcasted_iota(i32, (1, CHUNK), 1)
        own = jnp.where(slot < count_ref[0, 0], own, 0)
        limits.append((own, orbitals_of(kind_ref[:, at])))

    def products(step):
        at = spans[step]
        own, other = limits[step]
        levels = lax.broadcasted_iota(i32, (n_orbit, CHUNK), 0)
        ham = jnp.zeros((3, CHUNK), f32)
        ovl = ham
        for a in range(n_orbit):
            keep = levels < jnp.where(own > a, other, 0)
            weight_ref[a] = jnp.where(keep, density_ref[a, :, at].astype(f32), 0.0)
            energy_weight_ref[a] = jnp.where(keep, energy_ref[a, :, at].astype(f32), 0.0)
            for b in range(n_orbit):
                ham = ham + weight_ref[a, b : b + 1, :] * dham_ref[a, b, :, at].astype(f32)
                ovl = ovl + energy_weight_ref[a, b : b + 1, :] * dovl_ref[a, b, :, at].astype(f32)
        force_ref[:, at] = -2.0 * (ham - ovl)

    def scatter(step):
        at = spans[step]
        force = force_ref[:, at]
        high = force.astype(bf16).astype(f32)
        low = (force - high).astype(bf16).astype(f32)
        hot = lane_ref[:, at]
        spread = jnp.concatenate(
            [
                hot * jnp.broadcast_to(piece[c : c + 1, :], (LANES, CHUNK)).astype(bf16)
                for piece in (high, low)
                for c in range(3)
            ],
            axis=0,
        )
        new = product_nt(row_ref[:, at], spread)
        new = new[:, : 3 * LANES] + new[:, 3 * LANES :]
        blocks_at = lax.broadcasted_iota(i32, (blocks, CHUNK), 0) == owner_ref[:, at] // LANES
        own_rows = jnp.concatenate(
            [
                jnp.where(blocks_at, piece[c : c + 1, :], 0.0)
                for piece in (high, low)
                for c in range(3)
            ],
            axis=0,
        ).astype(bf16)
        own_new = product_nt(own_rows, own_lane_ref[:, at])
        if step == 0:
            total_ref[...] = new
            own_total_ref[...] = own_new
        else:
            total_ref[...] += new
            own_total_ref[...] += own_new

    for step in range(steps):
        for copy in streams[step]:
            copy.wait()
        if step + DEPTH < steps:
            for copy in streams[step + DEPTH]:
                copy.start()
        products(step)
        if step > 0:
            scatter(step - 1)
    scatter(steps - 1)
    for c in range(3):
        for q in range(blocks):
            sent_ref[pl.ds(c * blocks + q, owners, stride=3 * blocks), :] = -total_ref[
                q * owners : (q + 1) * owners, c * LANES : (c + 1) * LANES
            ]
    mine = lax.axis_index("atom") * (3 * blocks)
    for k in range(3 * blocks):
        at = pl.ds(mine + k, 1)
        own = own_total_ref[k : k + 1, :] + own_total_ref[3 * blocks + k : 3 * blocks + k + 1, :]
        sent_ref[at, :] = sent_ref[at, :] + own


def force_kernel(
    blocks, owners, images,
    image_ref, got_ref, now_ref, prior_ref, later_ref, first_ref, last_ref,
    force_ref, tangent_ref, parts_ref,
):
    is_first = image_ref[0] == 0
    is_last = image_ref[0] == images - 1
    zero = jnp.zeros((1, LANES), jnp.float32)
    ahead, behind, length, along = zero, zero, zero, zero
    for c in range(3):
        for q in range(blocks):
            k = c * blocks + q
            at = pl.ds(q * LANES, LANES)
            now = now_ref[c, :, at]
            prior = jnp.where(is_first, first_ref[c : c + 1, at], prior_ref[c, :, at])
            later = jnp.where(is_last, last_ref[c : c + 1, at], later_ref[c, :, at])
            tangent = later - prior
            got = got_ref[pl.ds(k, owners, stride=3 * blocks), :]
            force = jnp.sum(got, axis=0, keepdims=True)
            ahead = ahead + (later - now) ** 2
            behind = behind + (now - prior) ** 2
            length = length + tangent * tangent
            along = along + force * tangent
            force_ref[k : k + 1, :] = force
            tangent_ref[k : k + 1, :] = tangent
    place = lax.broadcasted_iota(jnp.int32, (1, LANES), 1)
    parts = zero
    for at, part in enumerate((ahead, behind, length, along)):
        parts = jnp.where(place == at, jnp.sum(part, axis=1, keepdims=True), parts)
    parts_ref[...] = jnp.broadcast_to(parts, parts_ref.shape)


def band_kernel(blocks, parts_ref, force_ref, tangent_ref, band_ref, along_ref):
    parts = jnp.sum(parts_ref[...], axis=0, keepdims=True)
    ahead, behind, length, along = (parts[:, at : at + 1] for at in range(4))
    root = jnp.sqrt(length + tangent_eps)
    along = along / root
    spring = spring_const * (jnp.sqrt(ahead) - jnp.sqrt(behind))
    push = spring - along
    for c in range(3):
        for q in range(blocks):
            k = c * blocks + q
            unit = tangent_ref[k : k + 1, :] / root
            band_ref[c, :, pl.ds(q * LANES, LANES)] = force_ref[k : k + 1, :] + push * unit
    along_ref[...] = jnp.broadcast_to(along, along_ref.shape)


def local(
    density,
    energy_density,
    dham,
    dovl,
    pair_owner,
    pair_partner,
    partner_species,
    pair_count,
    species,
    orbitals,
    coords,
    reactant,
    product,
):
    n_slots = density.shape[-1]
    n_orbit = density.shape[1]
    atoms_local = species.shape[0]
    blocks = atoms_local // LANES
    owners = lax.axis_size("atom")
    images = lax.axis_size("img")
    rows = 3 * blocks
    f32, i32 = jnp.float32, jnp.int32

    current = jnp.transpose(coords, (1, 0, 2))
    before = passed_along(current, "img", 1)
    after = passed_along(current, "img", -1)

    vmem, dma = pltpu.VMEM, pltpu.SemaphoreType.DMA
    bf16 = jnp.bfloat16
    sent = pl.pallas_call(
        lambda *refs: pairs_kernel(blocks, owners, *refs),
        out_shape=jax.ShapeDtypeStruct((owners * rows, LANES), f32),
        in_specs=[SMEM] + [HBM] * 9,
        out_specs=VMEM,
        scratch_shapes=[
            pltpu.SMEM(orbitals.shape, i32),
            vmem((blocks, LANES), i32),
            vmem((1, n_slots), i32),
            vmem((1, n_slots), i32),
            vmem((1, n_slots), i32),
            vmem((n_orbit, n_orbit, n_slots), bf16),
            vmem((n_orbit, n_orbit, n_slots), bf16),
            vmem((n_orbit, n_orbit, 3, n_slots), bf16),
            vmem((n_orbit, n_orbit, 3, n_slots), bf16),
            vmem((3, n_slots), f32),
            vmem((n_orbit, n_orbit, CHUNK), f32),
            vmem((n_orbit, n_orbit, CHUNK), f32),
            vmem((blocks * owners, n_slots), bf16),
            vmem((LANES, n_slots), bf16),
            vmem((LANES, n_slots), bf16),
            vmem((blocks * owners, 3 * LANES), f32),
            vmem((2 * rows, LANES), f32),
            dma((5,)),
            dma((4, n_slots // CHUNK)),
        ],
        compiler_params=pltpu.CompilerParams(vmem_limit_bytes=63 << 20),
        cost_estimate=cost(4 * n_slots * owners * rows * LANES, 8 * 243 * n_slots),
        name="pairs",
    )(
        pair_count,
        orbitals,
        species.reshape(blocks, LANES),
        pair_owner,
        pair_partner,
        partner_species,
        density,
        energy_density,
        jnp.transpose(dham, (0, 2, 3, 1, 4)),
        jnp.transpose(dovl, (0, 2, 3, 1, 4)),
    )
    got = lax.all_to_all(sent.reshape(owners, rows * LANES), "atom", 0, 0, tiled=True)

    force, tangent, parts = pl.pallas_call(
        lambda *refs: force_kernel(blocks, owners, images, *refs),
        out_shape=[
            jax.ShapeDtypeStruct((rows, LANES), f32),
            jax.ShapeDtypeStruct((rows, LANES), f32),
            jax.ShapeDtypeStruct((owners, LANES), f32),
        ],
        in_specs=[SMEM] + [VMEM] * 6,
        out_specs=[VMEM] * 3,
        compiler_params=pltpu.CompilerParams(vmem_limit_bytes=16 << 20),
        cost_estimate=cost(owners * rows * LANES, 4 * owners * rows * LANES),
        name="force",
    )(
        lax.axis_index("img").astype(i32).reshape(1),
        got.reshape(owners * rows, LANES),
        current,
        before,
        after,
        reactant,
        product,
    )
    parts = lax.all_to_all(parts, "atom", 0, 0, tiled=True)
    band, along = pl.pallas_call(
        lambda *refs: band_kernel(blocks, *refs),
        out_shape=[
            jax.ShapeDtypeStruct((3, 1, atoms_local), f32),
            jax.ShapeDtypeStruct((1, LANES), f32),
        ],
        in_specs=[VMEM] * 3,
        out_specs=[VMEM] * 2,
        compiler_params=pltpu.CompilerParams(vmem_limit_bytes=16 << 20),
        cost_estimate=cost(owners * LANES, 4 * owners * LANES),
        name="band",
    )(parts, force, tangent)
    return (jnp.transpose(band, (1, 0, 2)), along[0, :1])


def solution(mesh):
    return jax.shard_map(
        local,
        mesh=mesh,
        in_specs=(
            P("img", None, None, "atom"),
            P("img", None, None, "atom"),
            P("img", None, None, None, "atom"),
            P("img", None, None, None, "atom"),
            P("img", "atom"),
            P("img", "atom"),
            P("img", "atom"),
            P("img", "atom"),
            P("atom"),
            P(),
            P("img", None, "atom"),
            P(None, "atom"),
            P(None, "atom"),
        ),
        out_specs=(P("img", None, "atom"), P("img")),
        check_vma=False,
    )
```

```python
import jax
import jax.numpy as jnp
from jax import lax
from jax.experimental import pallas as pl
from jax.experimental.pallas import tpu as pltpu
from jax.sharding import PartitionSpec as P

spring_const = 1.0
tangent_eps = 1e-06
LANES = 128
CHUNK = 512
DEPTH = 2

VMEM = pl.BlockSpec(memory_space=pltpu.VMEM)
SMEM = pl.BlockSpec(memory_space=pltpu.SMEM)
HBM = pl.BlockSpec(memory_space=pltpu.HBM)


def cost(flops, moved):
    return pl.CostEstimate(flops=flops, bytes_accessed=moved, transcendentals=0)


def passed_along(block, axis, distance):
    devices = range(lax.axis_size(axis))
    route = [(i - distance, i) for i in devices if i - distance in devices]
    return lax.ppermute(block, axis, route)


def product_nt(a, b):
    return lax.dot_general(
        a, b, (((1,), (1,)), ((), ())), preferred_element_type=jnp.float32
    )


def pairs_kernel(
    blocks, owners,
    count_ref, orbitals_hbm, species_hbm, owner_hbm, partner_hbm, kind_hbm,
    density_hbm, energy_hbm, dham_hbm, dovl_hbm,
    sent_ref,
    orbitals_ref, species_ref, owner_ref, partner_ref, kind_ref,
    density_ref, energy_ref, dham_ref, dovl_ref,
    force_ref, weight_ref, energy_weight_ref, row_ref, lane_ref, own_lane_ref,
    total_ref, own_total_ref, level_ref, small_sem, block_sem,
):
    f32, bf16, i32 = jnp.float32, jnp.bfloat16, jnp.int32
    n_orbit, _, n_slots = density_ref.shape
    steps = n_slots // CHUNK
    small = [
        pltpu.make_async_copy(source, target, small_sem.at[i])
        for i, (source, target) in enumerate(
            (
                (orbitals_hbm, orbitals_ref),
                (species_hbm, species_ref),
                (owner_hbm, owner_ref),
                (partner_hbm, partner_ref),
                (kind_hbm, kind_ref),
            )
        )
    ]
    for copy in small:
        copy.start()
    spans = [pl.ds(step * CHUNK, CHUNK) for step in range(steps)]
    streams = []
    for step, at in enumerate(spans):
        pieces = (
            (density_hbm.at[0, :, :, at], density_ref.at[:, :, at]),
            (energy_hbm.at[0, :, :, at], energy_ref.at[:, :, at]),
            (dham_hbm.at[0, :, :, :, at], dham_ref.at[:, :, :, at]),
            (dovl_hbm.at[0, :, :, :, at], dovl_ref.at[:, :, :, at]),
        )
        streams.append(
            [
                pltpu.make_async_copy(source, target, block_sem.at[i, step])
                for i, (source, target) in enumerate(pieces)
            ]
        )
    for step in range(DEPTH):
        for copy in streams[step]:
            copy.start()
    for copy in small:
        copy.wait()

    def orbitals_of(kind):
        found = jnp.zeros_like(kind)
        for k in range(orbitals_ref.shape[0]):
            found = jnp.where(kind == k, orbitals_ref[k], found)
        return found

    table = orbitals_of(species_ref[...]).astype(f32)
    table = jnp.concatenate([table, jnp.zeros((8 - blocks, LANES), f32)], axis=0).astype(bf16)
    lane_bits = LANES.bit_length() - 1
    local_bits = (blocks * LANES).bit_length() - 1
    level_ref[...] = (
        lax.broadcasted_iota(i32, level_ref.shape, 0).astype(f32).astype(bf16)
    )
    one, zero = jnp.ones((), bf16), jnp.zeros((), bf16)
    limits = []
    for step, at in enumerate(spans):
        owner, partner = owner_ref[:, at], partner_ref[:, at]
        lanes = level_ref[:LANES, :]
        own_at = (owner & (LANES - 1)).astype(f32).astype(bf16)
        own_lane = jnp.where(lanes == own_at, one, zero)
        own_lane_ref[:, at] = own_lane
        partner_at = (partner & (LANES - 1)).astype(f32).astype(bf16)
        lane_ref[:, at] = jnp.where(lanes == partner_at, -one, zero)
        row = ((partner & (blocks * LANES - 1)) >> lane_bits) * owners + (partner >> local_bits)
        row_ref[:, at] = jnp.where(level_ref[...] == row.astype(f32).astype(bf16), one, zero)
        look = lax.dot_general(
            table, own_lane, (((1,), (0,)), ((), ())), preferred_element_type=f32
        )
        at_block = lax.broadcasted_iota(i32, (8, CHUNK), 0) == owner >> lane_bits
        own = jnp.sum(jnp.where(at_block, look, 0.0), axis=0, keepdims=True).astype(i32)
        slot = step * CHUNK + lax.broadcasted_iota(i32, (1, CHUNK), 1)
        own = jnp.where(slot < count_ref[0, 0], own, 0)
        limits.append((own, orbitals_of(kind_ref[:, at])))

    def products(step):
        at = spans[step]
        own, other = limits[step]
        levels = lax.broadcasted_iota(i32, (n_orbit, CHUNK), 0)
        ham = jnp.zeros((3, CHUNK), f32)
        ovl = ham
        for a in range(n_orbit):
            keep = levels < jnp.where(own > a, other, 0)
            weight_ref[a] = jnp.where(keep, density_ref[a, :, at].astype(f32), 0.0)
            energy_weight_ref[a] = jnp.where(keep, energy_ref[a, :, at].astype(f32), 0.0)
            for b in range(n_orbit):
                ham = ham + weight_ref[a, b : b + 1, :] * dham_ref[a, b, :, at].astype(f32)
                ovl = ovl + energy_weight_ref[a, b : b + 1, :] * dovl_ref[a, b, :, at].astype(f32)
        force_ref[:, at] = -2.0 * (ham - ovl)

    def scatter(step):
        at = spans[step]
        force = force_ref[:, at]
        high = force.astype(bf16).astype(f32)
        low = (force - high).astype(bf16).astype(f32)
        hot = lane_ref[:, at]
        spread = jnp.concatenate(
            [
                hot * jnp.broadcast_to(piece[c : c + 1, :], (LANES, CHUNK)).astype(bf16)
                for piece in (high, low)
                for c in range(3)
            ],
            axis=0,
        )
        new = product_nt(row_ref[:, at], spread)
        new = new[:, : 3 * LANES] + new[:, 3 * LANES :]
        blocks_at = lax.broadcasted_iota(i32, (blocks, CHUNK), 0) == owner_ref[:, at] >> lane_bits
        own_rows = jnp.concatenate(
            [
                jnp.where(blocks_at, piece[c : c + 1, :], 0.0)
                for piece in (high, low)
                for c in range(3)
            ],
            axis=0,
        ).astype(bf16)
        own_new = product_nt(own_rows, own_lane_ref[:, at])
        if step == 0:
            total_ref[...] = new
            own_total_ref[...] = own_new
        else:
            total_ref[...] += new
            own_total_ref[...] += own_new

    for step in range(steps):
        for copy in streams[step]:
            copy.wait()
        if step + DEPTH < steps:
            for copy in streams[step + DEPTH]:
                copy.start()
        products(step)
        if step > 0:
            scatter(step - 1)
    scatter(steps - 1)
    for c in range(3):
        for q in range(blocks):
            sent_ref[pl.ds(c * blocks + q, owners, stride=3 * blocks), :] = total_ref[
                q * owners : (q + 1) * owners, c * LANES : (c + 1) * LANES
            ]
    mine = lax.axis_index("atom") * (3 * blocks)
    for k in range(3 * blocks):
        at = pl.ds(mine + k, 1)
        own = own_total_ref[k : k + 1, :] + own_total_ref[3 * blocks + k : 3 * blocks + k + 1, :]
        sent_ref[at, :] = sent_ref[at, :] + own


def force_kernel(
    blocks, owners, images,
    image_ref, got_ref, now_ref, prior_ref, later_ref, first_ref, last_ref,
    force_ref, tangent_ref, parts_ref,
):
    is_first = image_ref[0] == 0
    is_last = image_ref[0] == images - 1
    zero = jnp.zeros((1, LANES), jnp.float32)
    ahead, behind, length, along = zero, zero, zero, zero
    for c in range(3):
        for q in range(blocks):
            k = c * blocks + q
            at = pl.ds(q * LANES, LANES)
            now = now_ref[c, :, at]
            prior = jnp.where(is_first, first_ref[c : c + 1, at], prior_ref[c, :, at])
            later = jnp.where(is_last, last_ref[c : c + 1, at], later_ref[c, :, at])
            tangent = later - prior
            got = got_ref[pl.ds(k, owners, stride=3 * blocks), :]
            force = jnp.sum(got, axis=0, keepdims=True)
            ahead = ahead + (later - now) ** 2
            behind = behind + (now - prior) ** 2
            length = length + tangent * tangent
            along = along + force * tangent
            force_ref[k : k + 1, :] = force
            tangent_ref[k : k + 1, :] = tangent
    place = lax.broadcasted_iota(jnp.int32, (1, LANES), 1)
    parts = zero
    for at, part in enumerate((ahead, behind, length, along)):
        parts = jnp.where(place == at, jnp.sum(part, axis=1, keepdims=True), parts)
    parts_ref[...] = jnp.broadcast_to(parts, parts_ref.shape)


def band_kernel(blocks, parts_ref, force_ref, tangent_ref, band_ref, along_ref):
    parts = jnp.sum(parts_ref[...], axis=0, keepdims=True)
    ahead, behind, length, along = (parts[:, at : at + 1] for at in range(4))
    root = jnp.sqrt(length + tangent_eps)
    along = along / root
    spring = spring_const * (jnp.sqrt(ahead) - jnp.sqrt(behind))
    push = spring - along
    for c in range(3):
        for q in range(blocks):
            k = c * blocks + q
            unit = tangent_ref[k : k + 1, :] / root
            band_ref[c, :, pl.ds(q * LANES, LANES)] = force_ref[k : k + 1, :] + push * unit
    along_ref[...] = jnp.broadcast_to(along, along_ref.shape)


def local(
    density,
    energy_density,
    dham,
    dovl,
    pair_owner,
    pair_partner,
    partner_species,
    pair_count,
    species,
    orbitals,
    coords,
    reactant,
    product,
):
    n_slots = density.shape[-1]
    n_orbit = density.shape[1]
    atoms_local = species.shape[0]
    blocks = atoms_local // LANES
    owners = lax.axis_size("atom")
    images = lax.axis_size("img")
    rows = 3 * blocks
    f32, i32 = jnp.float32, jnp.int32

    current = jnp.transpose(coords, (1, 0, 2))
    before = passed_along(current, "img", 1)
    after = passed_along(current, "img", -1)

    if (blocks * LANES) & (blocks * LANES - 1) or blocks * owners > 256:
        raise ValueError("sizes")
    vmem, dma = pltpu.VMEM, pltpu.SemaphoreType.DMA
    bf16 = jnp.bfloat16
    sent = pl.pallas_call(
        lambda *refs: pairs_kernel(blocks, owners, *refs),
        out_shape=jax.ShapeDtypeStruct((owners * rows, LANES), f32),
        in_specs=[SMEM] + [HBM] * 9,
        out_specs=VMEM,
        scratch_shapes=[
            pltpu.SMEM(orbitals.shape, i32),
            vmem((blocks, LANES), i32),
            vmem((1, n_slots), i32),
            vmem((1, n_slots), i32),
            vmem((1, n_slots), i32),
            vmem((n_orbit, n_orbit, n_slots), bf16),
            vmem((n_orbit, n_orbit, n_slots), bf16),
            vmem((n_orbit, n_orbit, 3, n_slots), bf16),
            vmem((n_orbit, n_orbit, 3, n_slots), bf16),
            vmem((3, n_slots), f32),
            vmem((n_orbit, n_orbit, CHUNK), f32),
            vmem((n_orbit, n_orbit, CHUNK), f32),
            vmem((blocks * owners, n_slots), bf16),
            vmem((LANES, n_slots), bf16),
            vmem((LANES, n_slots), bf16),
            vmem((blocks * owners, 3 * LANES), f32),
            vmem((2 * rows, LANES), f32),
            vmem((blocks * owners, CHUNK), bf16),
            dma((5,)),
            dma((4, n_slots // CHUNK)),
        ],
        compiler_params=pltpu.CompilerParams(vmem_limit_bytes=63 << 20),
        cost_estimate=cost(4 * n_slots * owners * rows * LANES, 8 * 243 * n_slots),
        name="pairs",
    )(
        pair_count,
        orbitals,
        species.reshape(blocks, LANES),
        pair_owner,
        pair_partner,
        partner_species,
        density,
        energy_density,
        jnp.transpose(dham, (0, 2, 3, 1, 4)),
        jnp.transpose(dovl, (0, 2, 3, 1, 4)),
    )
    got = lax.all_to_all(sent.reshape(owners, rows * LANES), "atom", 0, 0, tiled=True)

    force, tangent, parts = pl.pallas_call(
        lambda *refs: force_kernel(blocks, owners, images, *refs),
        out_shape=[
            jax.ShapeDtypeStruct((rows, LANES), f32),
            jax.ShapeDtypeStruct((rows, LANES), f32),
            jax.ShapeDtypeStruct((owners, LANES), f32),
        ],
        in_specs=[SMEM] + [VMEM] * 6,
        out_specs=[VMEM] * 3,
        compiler_params=pltpu.CompilerParams(vmem_limit_bytes=16 << 20),
        cost_estimate=cost(owners * rows * LANES, 4 * owners * rows * LANES),
        name="force",
    )(
        lax.axis_index("img").astype(i32).reshape(1),
        got.reshape(owners * rows, LANES),
        current,
        before,
        after,
        reactant,
        product,
    )
    parts = lax.all_to_all(parts, "atom", 0, 0, tiled=True)
    band, along = pl.pallas_call(
        lambda *refs: band_kernel(blocks, *refs),
        out_shape=[
            jax.ShapeDtypeStruct((3, 1, atoms_local), f32),
            jax.ShapeDtypeStruct((1, LANES), f32),
        ],
        in_specs=[VMEM] * 3,
        out_specs=[VMEM] * 2,
        compiler_params=pltpu.CompilerParams(vmem_limit_bytes=16 << 20),
        cost_estimate=cost(owners * LANES, 4 * owners * LANES),
        name="band",
    )(parts, force, tangent)
    return (jnp.transpose(band, (1, 0, 2)), along[0, :1])


def solution(mesh):
    return jax.shard_map(
        local,
        mesh=mesh,
        in_specs=(
            P("img", None, None, "atom"),
            P("img", None, None, "atom"),
            P("img", None, None, None, "atom"),
            P("img", None, None, None, "atom"),
            P("img", "atom"),
            P("img", "atom"),
            P("img", "atom"),
            P("img", "atom"),
            P("atom"),
            P(),
            P("img", None, "atom"),
            P(None, "atom"),
            P(None, "atom"),
        ),
        out_specs=(P("img", None, "atom"), P("img")),
        check_vma=False,
    )
```

```python
import jax
import jax.numpy as jnp
from jax import lax
from jax.experimental import pallas as pl
from jax.experimental.pallas import tpu as pltpu
from jax.sharding import PartitionSpec as P

spring_const = 1.0
tangent_eps = 1e-06
LANES = 128
CHUNK = 512
DEPTH = 2

VMEM = pl.BlockSpec(memory_space=pltpu.VMEM)
SMEM = pl.BlockSpec(memory_space=pltpu.SMEM)
HBM = pl.BlockSpec(memory_space=pltpu.HBM)


def cost(flops, moved):
    return pl.CostEstimate(flops=flops, bytes_accessed=moved, transcendentals=0)


def passed_along(block, axis, distance):
    devices = range(lax.axis_size(axis))
    route = [(i - distance, i) for i in devices if i - distance in devices]
    return lax.ppermute(block, axis, route)


def product_nt(a, b):
    return lax.dot_general(
        a, b, (((1,), (1,)), ((), ())), preferred_element_type=jnp.float32
    )


def pairs_kernel(
    blocks, owners,
    count_ref, orbitals_hbm, species_hbm, owner_hbm, partner_hbm, kind_hbm,
    density_hbm, energy_hbm, dham_hbm, dovl_hbm,
    sent_ref,
    orbitals_ref, species_ref, owner_ref, partner_ref, kind_ref,
    density_ref, energy_ref, dham_ref, dovl_ref,
    force_ref, weight_ref, energy_weight_ref, row_ref, lane_ref, own_lane_ref,
    total_ref, own_total_ref, level_ref, small_sem, block_sem,
):
    f32, bf16, i32 = jnp.float32, jnp.bfloat16, jnp.int32
    n_orbit, _, n_slots = density_ref.shape
    steps = n_slots // CHUNK
    small = [
        pltpu.make_async_copy(source, target, small_sem.at[i])
        for i, (source, target) in enumerate(
            (
                (orbitals_hbm, orbitals_ref),
                (species_hbm, species_ref),
                (owner_hbm, owner_ref),
                (partner_hbm, partner_ref),
                (kind_hbm, kind_ref),
            )
        )
    ]
    for copy in small:
        copy.start()
    spans = [pl.ds(step * CHUNK, CHUNK) for step in range(steps)]
    streams = []
    for step, at in enumerate(spans):
        pieces = (
            (density_hbm.at[0, :, :, at], density_ref.at[:, :, at]),
            (energy_hbm.at[0, :, :, at], energy_ref.at[:, :, at]),
            (dham_hbm.at[0, :, :, :, at], dham_ref.at[:, :, :, at]),
            (dovl_hbm.at[0, :, :, :, at], dovl_ref.at[:, :, :, at]),
        )
        streams.append(
            [
                pltpu.make_async_copy(source, target, block_sem.at[i, step])
                for i, (source, target) in enumerate(pieces)
            ]
        )
    for step in range(DEPTH):
        for copy in streams[step]:
            copy.start()
    for copy in small:
        copy.wait()

    def orbitals_of(kind):
        found = jnp.zeros_like(kind)
        for k in range(orbitals_ref.shape[0]):
            found = jnp.where(kind == k, orbitals_ref[k], found)
        return found

    table = orbitals_of(species_ref[...]).astype(f32)
    table = jnp.concatenate([table, jnp.zeros((8 - blocks, LANES), f32)], axis=0).astype(bf16)
    lane_bits = LANES.bit_length() - 1
    local_bits = (blocks * LANES).bit_length() - 1
    level_ref[...] = (
        lax.broadcasted_iota(i32, level_ref.shape, 0).astype(f32).astype(bf16)
    )
    one, zero = jnp.ones((), bf16), jnp.zeros((), bf16)
    limits = []
    for step, at in enumerate(spans):
        owner, partner = owner_ref[:, at], partner_ref[:, at]
        lanes = level_ref[:LANES, :]
        own_at = (owner & (LANES - 1)).astype(f32).astype(bf16)
        own_lane = jnp.where(lanes == own_at, one, zero)
        own_lane_ref[:, at] = own_lane
        partner_at = (partner & (LANES - 1)).astype(f32).astype(bf16)
        lane_ref[:, at] = jnp.where(lanes == partner_at, -one, zero)
        row = ((partner & (blocks * LANES - 1)) >> lane_bits) * owners + (partner >> local_bits)
        row_ref[:, at] = jnp.where(level_ref[...] == row.astype(f32).astype(bf16), one, zero)
        look = lax.dot_general(
            table, own_lane, (((1,), (0,)), ((), ())), preferred_element_type=f32
        )
        at_block = lax.broadcasted_iota(i32, (8, CHUNK), 0) == owner >> lane_bits
        own = jnp.sum(jnp.where(at_block, look, 0.0), axis=0, keepdims=True).astype(i32)
        slot = step * CHUNK + lax.broadcasted_iota(i32, (1, CHUNK), 1)
        own = jnp.where(slot < count_ref[0, 0], own, 0)
        limits.append((own, orbitals_of(kind_ref[:, at])))

    def products(step):
        at = spans[step]
        own, other = limits[step]
        levels = lax.broadcasted_iota(i32, (n_orbit, CHUNK), 0)
        ham = jnp.zeros((3, CHUNK), f32)
        ovl = ham
        for a in range(n_orbit):
            keep = levels < jnp.where(own > a, other, 0)
            weight_ref[a] = jnp.where(keep, density_ref[a, :, at].astype(f32), 0.0)
            energy_weight_ref[a] = jnp.where(keep, energy_ref[a, :, at].astype(f32), 0.0)
            for b in range(n_orbit):
                ham = ham + weight_ref[a, b : b + 1, :] * dham_ref[a, b, :, at].astype(f32)
                ovl = ovl + energy_weight_ref[a, b : b + 1, :] * dovl_ref[a, b, :, at].astype(f32)
        force_ref[:, at] = -2.0 * (ham - ovl)

    def scatter(step):
        at = spans[step]
        force = force_ref[:, at]
        high = force.astype(bf16).astype(f32)
        low = (force - high).astype(bf16).astype(f32)
        hot = lane_ref[:, at]
        spread = jnp.concatenate(
            [
                hot * jnp.broadcast_to(piece[c : c + 1, :], (LANES, CHUNK)).astype(bf16)
                for piece in (high, low)
                for c in range(3)
            ],
            axis=0,
        )
        new = product_nt(row_ref[:, at], spread)
        blocks_at = lax.broadcasted_iota(i32, (blocks, CHUNK), 0) == owner_ref[:, at] >> lane_bits
        own_rows = jnp.concatenate(
            [
                jnp.where(blocks_at, piece[c : c + 1, :], 0.0)
                for piece in (high, low)
                for c in range(3)
            ],
            axis=0,
        ).astype(bf16)
        own_new = product_nt(own_rows, own_lane_ref[:, at])
        if step == 0:
            total_ref[...] = new
            own_total_ref[...] = own_new
        else:
            total_ref[...] += new
            own_total_ref[...] += own_new

    for step in range(steps):
        for copy in streams[step]:
            copy.wait()
        if step + DEPTH < steps:
            for copy in streams[step + DEPTH]:
                copy.start()
        products(step)
        if step > 0:
            scatter(step - 1)
    scatter(steps - 1)
    for c in range(3):
        for q in range(blocks):
            from_rows = pl.ds(q * owners, owners)
            sent_ref[pl.ds(c * blocks + q, owners, stride=3 * blocks), :] = (
                total_ref[from_rows, c * LANES : (c + 1) * LANES]
                + total_ref[from_rows, (c + 3) * LANES : (c + 4) * LANES]
            )
    mine = lax.axis_index("atom") * (3 * blocks)
    for k in range(3 * blocks):
        at = pl.ds(mine + k, 1)
        own = own_total_ref[k : k + 1, :] + own_total_ref[3 * blocks + k : 3 * blocks + k + 1, :]
        sent_ref[at, :] = sent_ref[at, :] + own


def force_kernel(
    blocks, owners, images,
    image_ref, got_ref, now_ref, prior_ref, later_ref, first_ref, last_ref,
    force_ref, tangent_ref, parts_ref,
):
    is_first = image_ref[0] == 0
    is_last = image_ref[0] == images - 1
    zero = jnp.zeros((1, LANES), jnp.float32)
    ahead, behind, length, along = zero, zero, zero, zero
    for c in range(3):
        for q in range(blocks):
            k = c * blocks + q
            at = pl.ds(q * LANES, LANES)
            now = now_ref[c, :, at]
            prior = jnp.where(is_first, first_ref[c : c + 1, at], prior_ref[c, :, at])
            later = jnp.where(is_last, last_ref[c : c + 1, at], later_ref[c, :, at])
            tangent = later - prior
            got = got_ref[pl.ds(k, owners, stride=3 * blocks), :]
            force = jnp.sum(got, axis=0, keepdims=True)
            ahead = ahead + (later - now) ** 2
            behind = behind + (now - prior) ** 2
            length = length + tangent * tangent
            along = along + force * tangent
            force_ref[k : k + 1, :] = force
            tangent_ref[k : k + 1, :] = tangent
    place = lax.broadcasted_iota(jnp.int32, (1, LANES), 1)
    parts = zero
    for at, part in enumerate((ahead, behind, length, along)):
        parts = jnp.where(place == at, jnp.sum(part, axis=1, keepdims=True), parts)
    parts_ref[...] = jnp.broadcast_to(parts, parts_ref.shape)


def band_kernel(blocks, parts_ref, force_ref, tangent_ref, band_ref, along_ref):
    parts = jnp.sum(parts_ref[...], axis=0, keepdims=True)
    ahead, behind, length, along = (parts[:, at : at + 1] for at in range(4))
    root = jnp.sqrt(length + tangent_eps)
    along = along / root
    spring = spring_const * (jnp.sqrt(ahead) - jnp.sqrt(behind))
    push = spring - along
    for c in range(3):
        for q in range(blocks):
            k = c * blocks + q
            unit = tangent_ref[k : k + 1, :] / root
            band_ref[c, :, pl.ds(q * LANES, LANES)] = force_ref[k : k + 1, :] + push * unit
    along_ref[...] = jnp.broadcast_to(along, along_ref.shape)


def local(
    density,
    energy_density,
    dham,
    dovl,
    pair_owner,
    pair_partner,
    partner_species,
    pair_count,
    species,
    orbitals,
    coords,
    reactant,
    product,
):
    n_slots = density.shape[-1]
    n_orbit = density.shape[1]
    atoms_local = species.shape[0]
    blocks = atoms_local // LANES
    owners = lax.axis_size("atom")
    images = lax.axis_size("img")
    rows = 3 * blocks
    f32, i32 = jnp.float32, jnp.int32

    current = jnp.transpose(coords, (1, 0, 2))
    before = passed_along(current, "img", 1)
    after = passed_along(current, "img", -1)

    if (blocks * LANES) & (blocks * LANES - 1) or blocks * owners > 256:
        raise ValueError("sizes")
    vmem, dma = pltpu.VMEM, pltpu.SemaphoreType.DMA
    bf16 = jnp.bfloat16
    sent = pl.pallas_call(
        lambda *refs: pairs_kernel(blocks, owners, *refs),
        out_shape=jax.ShapeDtypeStruct((owners * rows, LANES), f32),
        in_specs=[SMEM] + [HBM] * 9,
        out_specs=VMEM,
        scratch_shapes=[
            pltpu.SMEM(orbitals.shape, i32),
            vmem((blocks, LANES), i32),
            vmem((1, n_slots), i32),
            vmem((1, n_slots), i32),
            vmem((1, n_slots), i32),
            vmem((n_orbit, n_orbit, n_slots), bf16),
            vmem((n_orbit, n_orbit, n_slots), bf16),
            vmem((n_orbit, n_orbit, 3, n_slots), bf16),
            vmem((n_orbit, n_orbit, 3, n_slots), bf16),
            vmem((3, n_slots), f32),
            vmem((n_orbit, n_orbit, CHUNK), f32),
            vmem((n_orbit, n_orbit, CHUNK), f32),
            vmem((blocks * owners, n_slots), bf16),
            vmem((LANES, n_slots), bf16),
            vmem((LANES, n_slots), bf16),
            vmem((blocks * owners, 6 * LANES), f32),
            vmem((2 * rows, LANES), f32),
            vmem((blocks * owners, CHUNK), bf16),
            dma((5,)),
            dma((4, n_slots // CHUNK)),
        ],
        compiler_params=pltpu.CompilerParams(vmem_limit_bytes=63 << 20),
        cost_estimate=cost(4 * n_slots * owners * rows * LANES, 8 * 243 * n_slots),
        name="pairs",
    )(
        pair_count,
        orbitals,
        species.reshape(blocks, LANES),
        pair_owner,
        pair_partner,
        partner_species,
        density,
        energy_density,
        jnp.transpose(dham, (0, 2, 3, 1, 4)),
        jnp.transpose(dovl, (0, 2, 3, 1, 4)),
    )
    got = lax.all_to_all(sent.reshape(owners, rows * LANES), "atom", 0, 0, tiled=True)

    force, tangent, parts = pl.pallas_call(
        lambda *refs: force_kernel(blocks, owners, images, *refs),
        out_shape=[
            jax.ShapeDtypeStruct((rows, LANES), f32),
            jax.ShapeDtypeStruct((rows, LANES), f32),
            jax.ShapeDtypeStruct((owners, LANES), f32),
        ],
        in_specs=[SMEM] + [VMEM] * 6,
        out_specs=[VMEM] * 3,
        compiler_params=pltpu.CompilerParams(vmem_limit_bytes=16 << 20),
        cost_estimate=cost(owners * rows * LANES, 4 * owners * rows * LANES),
        name="force",
    )(
        lax.axis_index("img").astype(i32).reshape(1),
        got.reshape(owners * rows, LANES),
        current,
        before,
        after,
        reactant,
        product,
    )
    parts = lax.all_to_all(parts, "atom", 0, 0, tiled=True)
    band, along = pl.pallas_call(
        lambda *refs: band_kernel(blocks, *refs),
        out_shape=[
            jax.ShapeDtypeStruct((3, 1, atoms_local), f32),
            jax.ShapeDtypeStruct((1, LANES), f32),
        ],
        in_specs=[VMEM] * 3,
        out_specs=[VMEM] * 2,
        compiler_params=pltpu.CompilerParams(vmem_limit_bytes=16 << 20),
        cost_estimate=cost(owners * LANES, 4 * owners * LANES),
        name="band",
    )(parts, force, tangent)
    return (jnp.transpose(band, (1, 0, 2)), along[0, :1])


def solution(mesh):
    return jax.shard_map(
        local,
        mesh=mesh,
        in_specs=(
            P("img", None, None, "atom"),
            P("img", None, None, "atom"),
            P("img", None, None, None, "atom"),
            P("img", None, None, None, "atom"),
            P("img", "atom"),
            P("img", "atom"),
            P("img", "atom"),
            P("img", "atom"),
            P("atom"),
            P(),
            P("img", None, "atom"),
            P(None, "atom"),
            P(None, "atom"),
        ),
        out_specs=(P("img", None, "atom"), P("img")),
        check_vma=False,
    )
```

```python
import jax
import jax.numpy as jnp
from jax import lax
from jax.experimental import pallas as pl
from jax.experimental.pallas import tpu as pltpu
from jax.sharding import PartitionSpec as P

spring_const = 1.0
tangent_eps = 1e-06
LANES = 128
CHUNK = 512
DEPTH = 2

VMEM = pl.BlockSpec(memory_space=pltpu.VMEM)
SMEM = pl.BlockSpec(memory_space=pltpu.SMEM)
HBM = pl.BlockSpec(memory_space=pltpu.HBM)


def cost(flops, moved):
    return pl.CostEstimate(flops=flops, bytes_accessed=moved, transcendentals=0)


def passed_along(block, axis, distance):
    devices = range(lax.axis_size(axis))
    route = [(i - distance, i) for i in devices if i - distance in devices]
    return lax.ppermute(block, axis, route)


def product_nt(a, b):
    return lax.dot_general(
        a, b, (((1,), (1,)), ((), ())), preferred_element_type=jnp.float32
    )


def pairs_kernel(
    blocks, owners,
    count_ref, orbitals_hbm, species_hbm, owner_hbm, partner_hbm, kind_hbm,
    density_hbm, energy_hbm, dham_hbm, dovl_hbm,
    sent_ref,
    orbitals_ref, species_ref, owner_ref, partner_ref, kind_ref,
    density_ref, energy_ref, dham_ref, dovl_ref,
    force_ref, weight_ref, energy_weight_ref, row_ref, lane_ref, own_lane_ref,
    total_ref, own_total_ref, level_ref, small_sem, block_sem,
):
    f32, bf16, i32 = jnp.float32, jnp.bfloat16, jnp.int32
    n_orbit, _, n_slots = density_ref.shape
    steps = n_slots // CHUNK
    small = [
        pltpu.make_async_copy(source, target, small_sem.at[i])
        for i, (source, target) in enumerate(
            (
                (orbitals_hbm, orbitals_ref),
                (species_hbm, species_ref),
                (owner_hbm, owner_ref),
                (partner_hbm, partner_ref),
                (kind_hbm, kind_ref),
            )
        )
    ]
    for copy in small:
        copy.start()
    spans = [pl.ds(step * CHUNK, CHUNK) for step in range(steps)]
    streams = []
    for step, at in enumerate(spans):
        pieces = (
            (density_hbm.at[0, :, :, at], density_ref.at[:, :, at]),
            (energy_hbm.at[0, :, :, at], energy_ref.at[:, :, at]),
            (dham_hbm.at[0, :, :, :, at], dham_ref.at[:, :, :, at]),
            (dovl_hbm.at[0, :, :, :, at], dovl_ref.at[:, :, :, at]),
        )
        streams.append(
            [
                pltpu.make_async_copy(source, target, block_sem.at[i, step])
                for i, (source, target) in enumerate(pieces)
            ]
        )
    for step in range(DEPTH):
        for copy in streams[step]:
            copy.start()
    for copy in small:
        copy.wait()

    def orbitals_of(kind):
        found = jnp.zeros_like(kind)
        for k in range(orbitals_ref.shape[0]):
            found = jnp.where(kind == k, orbitals_ref[k], found)
        return found

    table = orbitals_of(species_ref[...]).astype(f32)
    table = jnp.concatenate([table, jnp.zeros((8 - blocks, LANES), f32)], axis=0).astype(bf16)
    lane_bits = LANES.bit_length() - 1
    local_bits = (blocks * LANES).bit_length() - 1
    level_ref[...] = (
        lax.broadcasted_iota(i32, level_ref.shape, 0).astype(f32).astype(bf16)
    )
    one, zero = jnp.ones((), bf16), jnp.zeros((), bf16)
    limits = []

    def prepare(step):
        at = spans[step]
        owner, partner = owner_ref[:, at], partner_ref[:, at]
        lanes = level_ref[:LANES, :]
        own_at = (owner & (LANES - 1)).astype(f32).astype(bf16)
        own_lane = jnp.where(lanes == own_at, one, zero)
        own_lane_ref[:, at] = own_lane
        partner_at = (partner & (LANES - 1)).astype(f32).astype(bf16)
        lane_ref[:, at] = jnp.where(lanes == partner_at, -one, zero)
        row = ((partner & (blocks * LANES - 1)) >> lane_bits) * owners + (partner >> local_bits)
        row_ref[:, at] = jnp.where(level_ref[...] == row.astype(f32).astype(bf16), one, zero)
        look = lax.dot_general(
            table, own_lane, (((1,), (0,)), ((), ())), preferred_element_type=f32
        )
        at_block = lax.broadcasted_iota(i32, (8, CHUNK), 0) == owner >> lane_bits
        own = jnp.sum(jnp.where(at_block, look, 0.0), axis=0, keepdims=True).astype(i32)
        slot = step * CHUNK + lax.broadcasted_iota(i32, (1, CHUNK), 1)
        own = jnp.where(slot < count_ref[0, 0], own, 0)
        limits.append((own, orbitals_of(kind_ref[:, at])))

    def products(step):
        at = spans[step]
        own, other = limits[step]
        levels = lax.broadcasted_iota(i32, (n_orbit, CHUNK), 0)
        ham = jnp.zeros((3, CHUNK), f32)
        ovl = ham
        for a in range(n_orbit):
            keep = levels < jnp.where(own > a, other, 0)
            weight_ref[a] = jnp.where(keep, density_ref[a, :, at].astype(f32), 0.0)
            energy_weight_ref[a] = jnp.where(keep, energy_ref[a, :, at].astype(f32), 0.0)
            for b in range(n_orbit):
                ham = ham + weight_ref[a, b : b + 1, :] * dham_ref[a, b, :, at].astype(f32)
                ovl = ovl + energy_weight_ref[a, b : b + 1, :] * dovl_ref[a, b, :, at].astype(f32)
        force_ref[:, at] = -2.0 * (ham - ovl)

    def scatter(step):
        at = spans[step]
        force = force_ref[:, at]
        high = force.astype(bf16).astype(f32)
        low = (force - high).astype(bf16).astype(f32)
        hot = lane_ref[:, at]
        spread = jnp.concatenate(
            [
                hot * jnp.broadcast_to(piece[c : c + 1, :], (LANES, CHUNK)).astype(bf16)
                for piece in (high, low)
                for c in range(3)
            ],
            axis=0,
        )
        new = product_nt(row_ref[:, at], spread)
        blocks_at = lax.broadcasted_iota(i32, (blocks, CHUNK), 0) == owner_ref[:, at] >> lane_bits
        own_rows = jnp.concatenate(
            [
                jnp.where(blocks_at, piece[c : c + 1, :], 0.0)
                for piece in (high, low)
                for c in range(3)
            ],
            axis=0,
        ).astype(bf16)
        own_new = product_nt(own_rows, own_lane_ref[:, at])
        if step == 0:
            total_ref[...] = new
            own_total_ref[...] = own_new
        else:
            total_ref[...] += new
            own_total_ref[...] += own_new

    prepare(0)
    for step in range(steps):
        for copy in streams[step]:
            copy.wait()
        if step + DEPTH < steps:
            for copy in streams[step + DEPTH]:
                copy.start()
        products(step)
        if step + 1 < steps:
            prepare(step + 1)
        if step > 0:
            scatter(step - 1)
    scatter(steps - 1)
    for c in range(3):
        for q in range(blocks):
            from_rows = pl.ds(q * owners, owners)
            sent_ref[pl.ds(c * blocks + q, owners, stride=3 * blocks), :] = (
                total_ref[from_rows, c * LANES : (c + 1) * LANES]
                + total_ref[from_rows, (c + 3) * LANES : (c + 4) * LANES]
            )
    mine = lax.axis_index("atom") * (3 * blocks)
    for k in range(3 * blocks):
        at = pl.ds(mine + k, 1)
        own = own_total_ref[k : k + 1, :] + own_total_ref[3 * blocks + k : 3 * blocks + k + 1, :]
        sent_ref[at, :] = sent_ref[at, :] + own


def force_kernel(
    blocks, owners, images,
    image_ref, got_ref, now_ref, prior_ref, later_ref, first_ref, last_ref,
    force_ref, tangent_ref, parts_ref,
):
    is_first = image_ref[0] == 0
    is_last = image_ref[0] == images - 1
    zero = jnp.zeros((1, LANES), jnp.float32)
    ahead, behind, length, along = zero, zero, zero, zero
    for c in range(3):
        for q in range(blocks):
            k = c * blocks + q
            at = pl.ds(q * LANES, LANES)
            now = now_ref[c, :, at]
            prior = jnp.where(is_first, first_ref[c : c + 1, at], prior_ref[c, :, at])
            later = jnp.where(is_last, last_ref[c : c + 1, at], later_ref[c, :, at])
            tangent = later - prior
            got = got_ref[pl.ds(k, owners, stride=3 * blocks), :]
            force = jnp.sum(got, axis=0, keepdims=True)
            ahead = ahead + (later - now) ** 2
            behind = behind + (now - prior) ** 2
            length = length + tangent * tangent
            along = along + force * tangent
            force_ref[k : k + 1, :] = force
            tangent_ref[k : k + 1, :] = tangent
    place = lax.broadcasted_iota(jnp.int32, (1, LANES), 1)
    parts = zero
    for at, part in enumerate((ahead, behind, length, along)):
        parts = jnp.where(place == at, jnp.sum(part, axis=1, keepdims=True), parts)
    parts_ref[...] = jnp.broadcast_to(parts, parts_ref.shape)


def band_kernel(blocks, parts_ref, force_ref, tangent_ref, band_ref, along_ref):
    parts = jnp.sum(parts_ref[...], axis=0, keepdims=True)
    ahead, behind, length, along = (parts[:, at : at + 1] for at in range(4))
    root = jnp.sqrt(length + tangent_eps)
    along = along / root
    spring = spring_const * (jnp.sqrt(ahead) - jnp.sqrt(behind))
    push = spring - along
    for c in range(3):
        for q in range(blocks):
            k = c * blocks + q
            unit = tangent_ref[k : k + 1, :] / root
            band_ref[c, :, pl.ds(q * LANES, LANES)] = force_ref[k : k + 1, :] + push * unit
    along_ref[...] = jnp.broadcast_to(along, along_ref.shape)


def local(
    density,
    energy_density,
    dham,
    dovl,
    pair_owner,
    pair_partner,
    partner_species,
    pair_count,
    species,
    orbitals,
    coords,
    reactant,
    product,
):
    n_slots = density.shape[-1]
    n_orbit = density.shape[1]
    atoms_local = species.shape[0]
    blocks = atoms_local // LANES
    owners = lax.axis_size("atom")
    images = lax.axis_size("img")
    rows = 3 * blocks
    f32, i32 = jnp.float32, jnp.int32

    current = jnp.transpose(coords, (1, 0, 2))
    before = passed_along(current, "img", 1)
    after = passed_along(current, "img", -1)

    if (blocks * LANES) & (blocks * LANES - 1) or blocks * owners > 256:
        raise ValueError("sizes")
    vmem, dma = pltpu.VMEM, pltpu.SemaphoreType.DMA
    bf16 = jnp.bfloat16
    sent = pl.pallas_call(
        lambda *refs: pairs_kernel(blocks, owners, *refs),
        out_shape=jax.ShapeDtypeStruct((owners * rows, LANES), f32),
        in_specs=[SMEM] + [HBM] * 9,
        out_specs=VMEM,
        scratch_shapes=[
            pltpu.SMEM(orbitals.shape, i32),
            vmem((blocks, LANES), i32),
            vmem((1, n_slots), i32),
            vmem((1, n_slots), i32),
            vmem((1, n_slots), i32),
            vmem((n_orbit, n_orbit, n_slots), bf16),
            vmem((n_orbit, n_orbit, n_slots), bf16),
            vmem((n_orbit, n_orbit, 3, n_slots), bf16),
            vmem((n_orbit, n_orbit, 3, n_slots), bf16),
            vmem((3, n_slots), f32),
            vmem((n_orbit, n_orbit, CHUNK), f32),
            vmem((n_orbit, n_orbit, CHUNK), f32),
            vmem((blocks * owners, n_slots), bf16),
            vmem((LANES, n_slots), bf16),
            vmem((LANES, n_slots), bf16),
            vmem((blocks * owners, 6 * LANES), f32),
            vmem((2 * rows, LANES), f32),
            vmem((blocks * owners, CHUNK), bf16),
            dma((5,)),
            dma((4, n_slots // CHUNK)),
        ],
        compiler_params=pltpu.CompilerParams(vmem_limit_bytes=63 << 20),
        cost_estimate=cost(4 * n_slots * owners * rows * LANES, 8 * 243 * n_slots),
        name="pairs",
    )(
        pair_count,
        orbitals,
        species.reshape(blocks, LANES),
        pair_owner,
        pair_partner,
        partner_species,
        density,
        energy_density,
        jnp.transpose(dham, (0, 2, 3, 1, 4)),
        jnp.transpose(dovl, (0, 2, 3, 1, 4)),
    )
    got = lax.all_to_all(sent.reshape(owners, rows * LANES), "atom", 0, 0, tiled=True)

    force, tangent, parts = pl.pallas_call(
        lambda *refs: force_kernel(blocks, owners, images, *refs),
        out_shape=[
            jax.ShapeDtypeStruct((rows, LANES), f32),
            jax.ShapeDtypeStruct((rows, LANES), f32),
            jax.ShapeDtypeStruct((owners, LANES), f32),
        ],
        in_specs=[SMEM] + [VMEM] * 6,
        out_specs=[VMEM] * 3,
        compiler_params=pltpu.CompilerParams(vmem_limit_bytes=16 << 20),
        cost_estimate=cost(owners * rows * LANES, 4 * owners * rows * LANES),
        name="force",
    )(
        lax.axis_index("img").astype(i32).reshape(1),
        got.reshape(owners * rows, LANES),
        current,
        before,
        after,
        reactant,
        product,
    )
    parts = lax.all_to_all(parts, "atom", 0, 0, tiled=True)
    band, along = pl.pallas_call(
        lambda *refs: band_kernel(blocks, *refs),
        out_shape=[
            jax.ShapeDtypeStruct((3, 1, atoms_local), f32),
            jax.ShapeDtypeStruct((1, LANES), f32),
        ],
        in_specs=[VMEM] * 3,
        out_specs=[VMEM] * 2,
        compiler_params=pltpu.CompilerParams(vmem_limit_bytes=16 << 20),
        cost_estimate=cost(owners * LANES, 4 * owners * LANES),
        name="band",
    )(parts, force, tangent)
    return (jnp.transpose(band, (1, 0, 2)), along[0, :1])


def solution(mesh):
    return jax.shard_map(
        local,
        mesh=mesh,
        in_specs=(
            P("img", None, None, "atom"),
            P("img", None, None, "atom"),
            P("img", None, None, None, "atom"),
            P("img", None, None, None, "atom"),
            P("img", "atom"),
            P("img", "atom"),
            P("img", "atom"),
            P("img", "atom"),
            P("atom"),
            P(),
            P("img", None, "atom"),
            P(None, "atom"),
            P(None, "atom"),
        ),
        out_specs=(P("img", None, "atom"), P("img")),
        check_vma=False,
    )
```
